256 devices in a mesh: panel: 16 (over x, y), front: 16 (over z, core).
Axes of the slice: x: 4, y: 4, z: 8, core: 2. Of those that a mesh axis runs over, the one named last changes fastest.
Arguments:
- leaf_inv: float32 [16, 16, 768, 768], P('panel', 'front'), may hold values from -0.21875 to 0.21875
- parent_inv: float32 [16, 16, 768, 768], P('panel', 'front'), may hold values from -0.21875 to 0.21875
- up_coupling: float32 [16, 16, 384, 768], P('panel', 'front'), may hold values from -0.21875 to 0.21875
- down_coupling: float32 [16, 16, 768, 384], P('panel', 'front'), may hold values from -0.3125 to 0.3125
- interface_coupling: float32 [16, 16, 768, 512], P('panel', 'front'), may hold values from -0.25 to 0.25
- leaf_sources: float32 [16, 16, 3, 768, 128], P('panel', 'front'), may hold values from -6 to 6
- parent_sources: float32 [16, 16, 3, 768, 128], P('panel', 'front'), may hold values from -6 to 6
- parent_of: int32 [16, 16], P('panel'), may hold values from 0 to 15
- update_count: int32 [16, 16], P('panel'), may hold values from 128 to 384, as said below
- update_rows: int32 [16, 16, 384], P('panel'), may hold values from 0 to 767, as said below
Outputs:
- leaf_solution: float32 [16, 16, 3, 768, 128], P('panel', 'front')
- parent_solution: float32 [16, 16, 3, 768, 128], P('panel', 'front')
The draws below stay inside these ranges and needn't reach their ends.
Inputs may be any that keep to these rules, and one draw needn't show every extreme that they name: `update_count`: a multiple of 128; some leaf of every panel has 384. `update_rows`: the entries of one leaf are distinct; those at or past its update_count are padding.
All inputs are finite; a program needn't handle non-finite values.
Results may differ from the reference program's by a relative error of at most 0.0003.
Values sent between devices are 32-bit elements; how exact they have to be, the bound alone decides.
A program may use at most 128 MiB of HBM per device.

```python
import math
import jax
import jax.numpy as jnp
import numpy as np
from jax import lax

LEAF = 768
PARENT = 768
BLOCK = 128
UPDATE_BLOCKS = 3
IFACE = 512
SOURCES = 128
TICKS = 3
UMAX = 384
N_PANEL = 16
N_FRONT = 16


def draw_update_count(key, part):
    first_key = jax.random.fold_in(key, 11)
    second_key = jax.random.fold_in(key, 12)
    blocks = jax.random.randint(first_key, (N_PANEL, N_FRONT), 1, UPDATE_BLOCKS + 1)
    fullest = jax.random.randint(second_key, (N_PANEL, 1), 0, N_FRONT)
    positions = jnp.arange(N_FRONT)[None, :]
    blocks = jnp.where(positions == fullest, UPDATE_BLOCKS, blocks)
    return (blocks * BLOCK).astype(jnp.int32)


def leading_rows(subkey):
    return jax.random.permutation(subkey, PARENT)[:UMAX]


def draw_update_rows(key, part):
    subkeys = jax.random.split(jax.random.fold_in(key, 21), N_PANEL * N_FRONT)
    chosen = jax.vmap(leading_rows)(subkeys)
    return chosen.reshape(N_PANEL, N_FRONT, UMAX).astype(jnp.int32)


def with_ends(result, own_key, least, largest):
    shape = result.shape
    place = [jax.random.randint(jax.random.fold_in(own_key, axis), (), 0, shape[axis]) for axis in range(len(shape))]
    result = result.at[tuple(place)].set(least)
    longest = shape.index(max(shape))
    place[longest] = (place[longest] + 1) % shape[longest]
    return result.at[tuple(place)].set(largest)


def shard_levels(key, shape, cuts, low, largest):
    def one(axis_at, parts):
        heights = jax.random.uniform(jax.random.fold_in(jax.random.fold_in(key, 6), axis_at), (parts,), jnp.float32, low / len(cuts), largest / len(cuts))
        return jnp.repeat(jnp.exp(heights), shape[axis_at] // parts).reshape((-1,) + (1,) * (len(shape) - axis_at - 1))

    factor_of = one(*cuts[0])
    for cut in cuts[1:]:
        factor_of = factor_of * one(*cut)
    return factor_of


def rank_bounds(count, lean):
    weights = [(1 << 20) // math.isqrt(rank ** lean) + 1 for rank in range(1, count + 1)]
    scale = 1 + sum(weights) // (1 << 30)
    return np.cumsum(np.array([max(1, weight // scale) for weight in weights]))


def skewed_ids(own_key, shape, number_of, skew):
    grid = rank_bounds(number_of, skew)
    ticket = jax.random.randint(jax.random.fold_in(own_key, 1), shape, 0, int(grid[number_of - 1]))
    rank = jnp.searchsorted(jnp.asarray(grid, jnp.int32), ticket, side="right")
    return jax.random.permutation(jax.random.fold_in(own_key, 2), number_of)[rank].astype(jnp.int32)


def gaussian(stream_key, dims, spread, bound, pieces=(), held_as=jnp.bfloat16):
    array = jax.random.normal(stream_key, dims, jnp.float32) * spread
    if len(pieces) > 0:
        array = shard_levels(stream_key, dims, pieces, -0.22, 0.18) * array
    return jnp.clip(array, min=-bound, max=bound).astype(held_as)


def setup_inputs(seed: int = 0) -> dict:
    arg_keys = jax.random.split(jax.random.key(seed), 11)
    leaf_inv = gaussian(arg_keys[0], (N_PANEL, N_FRONT, LEAF, LEAF), LEAF ** -0.5, 0.21875, ((0, 16), (1, 16)), jnp.float32)
    parent_inv = gaussian(arg_keys[1], (N_PANEL, N_FRONT, PARENT, PARENT), PARENT ** -0.5, 0.21875, ((0, 16), (1, 16)), jnp.float32)
    up_coupling = gaussian(arg_keys[2], (N_PANEL, N_FRONT, UMAX, LEAF), LEAF ** -0.5, 0.21875, ((0, 16), (1, 16)), jnp.float32)
    down_coupling = gaussian(arg_keys[3], (N_PANEL, N_FRONT, LEAF, UMAX), UMAX ** -0.5, 0.3125, ((0, 16), (1, 16)), jnp.float32)
    interface_coupling = gaussian(arg_keys[4], (N_PANEL, N_FRONT, LEAF, IFACE), IFACE ** -0.5, 0.25, ((0, 16), (1, 16)), jnp.float32)
    leaf_sources = gaussian(arg_keys[5], (N_PANEL, N_FRONT, TICKS, LEAF, SOURCES), 1.0, 6.0, ((0, 16), (1, 16)), jnp.float32)
    parent_sources = gaussian(arg_keys[6], (N_PANEL, N_FRONT, TICKS, PARENT, SOURCES), 1.0, 6.0, ((0, 16), (1, 16)), jnp.float32)
    parent_of = with_ends(skewed_ids(arg_keys[7], (N_PANEL, N_FRONT), N_FRONT, 2), jax.random.fold_in(arg_keys[7], 3), 0, N_FRONT - 1).astype(jnp.int32)
    update_count = draw_update_count(jax.random.fold_in(arg_keys[10], 71), 0)
    update_rows = draw_update_rows(jax.random.fold_in(arg_keys[10], 71), 0)
    return {"leaf_inv": leaf_inv, "parent_inv": parent_inv, "up_coupling": up_coupling, "down_coupling": down_coupling, "interface_coupling": interface_coupling, "leaf_sources": leaf_sources, "parent_sources": parent_sources, "parent_of": parent_of, "update_count": update_count, "update_rows": update_rows}


highest_precision = lax.Precision.HIGHEST


def apply_front(matrix, operand):
    return jnp.einsum("pfij,pfjb->pfib", matrix, operand, precision=highest_precision)


def assemble_panel(update, parents, counts, row_ids):
    fronts, update_cap, columns = update.shape
    live_slots = jnp.arange(update_cap, dtype=jnp.int32)[None, :] < counts[:, None]
    targets = jnp.where(live_slots, parents[:, None] * PARENT + row_ids, fronts * PARENT).astype(jnp.int32)
    summed = jax.ops.segment_sum(update.reshape(fronts * update_cap, columns), targets.reshape(-1), num_segments=fronts * PARENT + 1)
    return summed[:fronts * PARENT].reshape(fronts, PARENT, columns)


def descend_panel(solved, parents, counts, row_ids):
    fronts, parent_order, columns = solved.shape
    update_cap = row_ids.shape[1]
    flattened = solved.reshape(fronts * parent_order, columns)
    take_index = (parents[:, None] * parent_order + row_ids).reshape(-1).astype(jnp.int32)
    picked = jnp.take(flattened, take_index, axis=0).reshape(fronts, update_cap, columns)
    live_slots = jnp.arange(update_cap, dtype=jnp.int32)[None, :] < counts[:, None]
    return jnp.where(live_slots[:, :, None], picked, 0.0)


def reference(leaf_inv, parent_inv, up_coupling, down_coupling, interface_coupling, leaf_sources, parent_sources, parent_of, update_count, update_rows):
    live_slots = jnp.arange(UMAX, dtype=jnp.int32)[None, None, :] < update_count[:, :, None]
    previous = None
    leaf_list = []
    parent_list = []
    for tick_index in range(TICKS):
        sources = leaf_sources[:, :, tick_index]
        if tick_index == 0:
            leaf_rhs = sources
        else:
            edge = previous[:, :, LEAF - IFACE:, :]
            interface = jnp.concatenate([jnp.zeros_like(edge[:1]), edge[:-1]], axis=0)
            leaf_rhs = sources + apply_front(interface_coupling, interface)
        partial_solution = apply_front(leaf_inv, leaf_rhs)
        update = jnp.where(live_slots[..., None], apply_front(up_coupling, partial_solution), 0.0)
        assembled = jax.vmap(assemble_panel)(update, parent_of, update_count, update_rows)
        solved = apply_front(parent_inv, parent_sources[:, :, tick_index] - assembled)
        descended = jax.vmap(descend_panel)(solved, parent_of, update_count, update_rows)
        leaf_now = partial_solution - apply_front(down_coupling, descended)
        leaf_list.append(leaf_now)
        parent_list.append(solved)
        previous = leaf_now
    return jnp.stack(leaf_list, axis=2), jnp.stack(parent_list, axis=2)
```

```python
import functools

import jax
import jax.numpy as jnp
from jax import lax
from jax.experimental import pallas as pl
from jax.experimental.pallas import tpu as pltpu
from jax.sharding import PartitionSpec as P

F32 = jnp.float32
BF16 = jnp.bfloat16
MESH = pl.DeviceIdType.MESH
HALVES = 1


def dot(a, b):
    return jnp.dot(a, b, preferred_element_type=F32)


def split(x):
    hi = x.astype(BF16)
    return hi, (x - hi.astype(F32)).astype(BF16)


def kernel(
    cfg,
    li_hbm, pi_hbm, up_hbm, dn_hbm, ic_hbm, ls_hbm, ps_hbm, par_ref, cnt_ref, row_ref,
    leaf_hbm, par_hbm,
    LI, PI, UP, DN, IC, LS, PS,
    LIh, LIl, PIh, PIl, UPh, UPl, DNh, DNl, ICh, ICl, Mh, Ml, M2h, M2l,
    V, W, S, T, TG, UB, RB, SB, PXS, PXR, SXS, SXR, XS, XR, ACC, RG, PART, LO, PO,
    ld_sem, st_sem, up_s, up_r, dn_s, dn_r, px_sem, sx_sem, x_s, x_r,
):
    n_panel, n_front, ticks, H = cfg
    nz = n_front // 2
    dm = nz // 2
    N, C = LS.shape[1:]
    U = UP.shape[0]
    Q = IC.shape[1]
    pr = U // H
    nch = 4 // H
    cr = pr // nch
    hc = C // 2
    panel = lax.axis_index("panel")
    front = lax.axis_index("front")
    z = front // 2
    core = lax.rem(front, 2)
    mate = front + 1 - 2 * core

    def zslot(d):
        return lax.rem(z + d + nz, nz)

    def zdev(d):
        return {"front": 2 * zslot(d) + core}

    loads = []
    for i, (src, dst) in enumerate(
        [
            (li_hbm.at[0, 0], LI), (ls_hbm.at[0, 0], LS), (up_hbm.at[0, 0], UP), (ic_hbm.at[0, 0], IC),
            (ps_hbm.at[0, 0], PS), (pi_hbm.at[0, 0], PI), (dn_hbm.at[0, 0], DN),
        ]
    ):
        loads.append(pltpu.make_async_copy(src, dst, ld_sem.at[i]))
        loads[-1].start()
    barrier = pltpu.get_barrier_semaphore()
    for who in (
        zdev(1), zdev(-1), {"front": mate},
        {"panel": lax.rem(panel + 1, n_panel)}, {"panel": lax.rem(panel + n_panel - 1, n_panel)},
    ):
        pl.semaphore_signal(barrier, inc=1, device_id=who, device_id_type=MESH)

    def low(shape):
        return lax.broadcasted_iota(jnp.int32, shape, 1) < hc

    def swap(x):
        return pltpu.roll(x, hc, 1)

    def half(x, h):
        if H == 1:
            return x
        return jnp.where(low(x.shape), x, swap(x)) if h == 0 else jnp.where(low(x.shape), swap(x), x)

    def pack(x):
        if H == 1:
            return x
        m = x.shape[0] // 2
        return jnp.where(low((m, C)), x[:m], x[m:])

    def unpack(p):
        if H == 1:
            return p
        m, s = low(p.shape), swap(p)
        return jnp.concatenate([jnp.where(m, p, s), jnp.where(m, s, p)], axis=0)

    def rhs1(x):
        if H == 1:
            return jnp.concatenate(split(x), axis=1)
        hi = x.astype(BF16).astype(F32)
        return jnp.where(low(x.shape), hi, x - hi).astype(BF16)

    def rhs2(x):
        if H == 1:
            return x.astype(BF16)
        return jnp.where(low(x.shape), x, 0.0).astype(BF16)

    def fin(o):
        if H == 1:
            return o[:, :C] + o[:, C:]
        return o + swap(o)

    def mm3(ah, al, x):
        if H == 1:
            return fin(dot(ah, rhs1(x))) + dot(al, rhs2(x))
        return fin(dot(ah, rhs1(x)) + dot(al, rhs2(x)))

    def mm3_full(ah, al, x):
        xh, xl = split(x)
        o = dot(ah, jnp.concatenate([xh, xl], axis=1))
        return o[:, :C] + o[:, C:] + dot(al, xh)

    def mmm(ah, al, bh, bl):
        return dot(ah, bh) + dot(ah, bl) + dot(al, bh)

    done = set()

    def once(key, fn):
        if key not in done:
            done.add(key)
            fn()

    def load(i, full, hi, lo):
        def go():
            loads[i].wait()
            h, l = split(full[...])
            hi[...] = h
            lo[...] = l
        once(("load", i), go)

    def need_l():
        load(0, LI, LIh, LIl)

    def need_ls():
        once("ls", lambda: loads[1].wait())

    def need_u():
        load(2, UP, UPh, UPl)

    def need_ps():
        once("ps", lambda: loads[4].wait())

    def need_p():
        load(5, PI, PIh, PIl)

    def need_d():
        load(6, DN, DNh, DNl)

    def need_v(t):
        def go():
            need_l()
            need_ls()
            V[t] = mm3_full(LIh[...], LIl[...], LS[t])
        once(("v", t), go)

    def need_w(t):
        def go():
            need_v(t)
            need_u()
            W[t] = mm3_full(UPh[...], UPl[...], V[t])
        once(("w", t), go)

    def need_m():
        def go():
            load(3, IC, ICh, ICl)
            need_l()
            h, l = split(mmm(LIh[...], LIl[...], ICh[...], ICl[...]))
            Mh[...] = h
            Ml[...] = l
        once("m", go)

    def need_m2():
        def go():
            need_m()
            need_u()
            h, l = split(mmm(UPh[...], UPl[...], Mh[...], Ml[...]))
            M2h[...] = h
            M2l[...] = l
        once("m2", go)

    def need_tg():
        def go():
            k = lax.broadcasted_iota(jnp.int32, (1, U), 1)
            for w in range(nz):
                leaf = 2 * w + core
                rows = row_ref[0, pl.ds(leaf, 1), :]
                par = jnp.full((1, U), par_ref[0, leaf], jnp.int32)
                cnt = jnp.full((1, U), cnt_ref[0, leaf], jnp.int32)
                there = jnp.where(par == front, rows, jnp.where(par == mate, rows + N, -1))
                TG[pl.ds(w, 1), :] = jnp.where(k < cnt, there, -1)
        once("tg", go)

    def need_s(d):
        def go():
            need_tg()
            w = zslot(d)
            tgt = TG[pl.ds(w, 1), :]
            i = lax.broadcasted_iota(jnp.int32, (2 * N, U), 0)
            S[w] = jnp.where(i == tgt, 1.0, 0.0).astype(BF16)
        once(("s", d % nz), go)

    def need_t(w):
        def go():
            need_tg()
            col = jnp.transpose(TG[...])[:, w : w + 1]
            i = lax.broadcasted_iota(jnp.int32, (U, 2 * N), 1)
            T[w] = jnp.where(i == col, 1.0, 0.0).astype(BF16)
        once(("t", w), go)

    def in_half(d, c):
        return c < nch // 2 if d == 0 else c >= nch // 2

    def up_copy(h, d, k, c):
        sgn = 1 if d == 0 else -1
        ref = UB.at[h, zslot(-sgn * k), pl.ds(c * cr, cr)]
        return pltpu.make_async_remote_copy(
            ref, ref, up_s.at[h, d, k, c], up_r.at[h, d, k, c], device_id=zdev(sgn), device_id_type=MESH
        )

    def up_arrival(h, d, k, c):
        sgn = 1 if d == 0 else -1
        ref = UB.at[h, zslot(-sgn * (k + 1)), pl.ds(c * cr, cr)]
        return pltpu.make_async_remote_copy(
            ref, ref, up_s.at[h, d, k, c], up_r.at[h, d, k, c], device_id=zdev(sgn), device_id_type=MESH
        )

    def dn_copy(h, d, k, c):
        sgn = 1 if d == 0 else -1
        at = pl.ds(c * cr, cr)
        return pltpu.make_async_remote_copy(
            SB.at[h, d, k, at], RB.at[h, d, k, at], dn_s.at[h, d, k, c], dn_r.at[h, d, k, c],
            device_id=zdev(sgn), device_id_type=MESH,
        )

    def mate_copy(src, dst, sem, h):
        return pltpu.make_async_remote_copy(
            src.at[h], dst.at[h], sem.at[h, 0], sem.at[h, 1], device_id={"front": mate}, device_id_type=MESH
        )

    def x_copy(h, t):
        return pltpu.make_async_remote_copy(
            XS.at[h], XR.at[h, t], x_s.at[h], x_r.at[h, t],
            device_id={"panel": lax.rem(panel + 1, n_panel)}, device_id_type=MESH,
        )

    def chunks(k):
        for c in range(nch):
            for d in range(2):
                if k < dm - 1 or in_half(d, c):
                    yield d, c

    def out_copy(src, dst, i, t):
        return pltpu.make_async_copy(src.at[t], dst.at[0, 0, t], st_sem.at[i, t])

    def sel(h, w):
        return pack(fin(dot(T[w], RG[h])))

    def sweep(h):
        for t in range(ticks):
            if t == 0:
                need_w(0)
                u = half(W[0], h)
            else:
                need_m2()
                need_w(t)
                x_copy(h, t - 1).wait_recv()
                x = jnp.where(panel > 0, unpack(XR[h, t - 1]), 0.0)
                u = half(W[t], h) + mm3(M2h[...], M2l[...], x)
            UB[h, z] = pack(u)
            if t == 0:
                once("barrier", lambda: pl.semaphore_wait(barrier, 5))
            for d, c in chunks(0):
                up_copy(h, d, 0, c).start()
            yield
            need_s(0)
            ACC[h] = dot(S[z], rhs1(u))
            if t == 0:
                need_v(0)
                PART[h] = half(V[0], h)
            else:
                need_m()
                need_v(t)
                PART[h] = half(V[t], h) + mm3(Mh[...], Ml[...], x)
            yield
            for k in range(1, dm + 1):
                for d, c in chunks(k - 1):
                    up_arrival(h, d, k - 1, c).wait_recv()
                    if k < dm and (k < dm - 1 or in_half(d, c)):
                        up_copy(h, d, k, c).start()
                yield
                for w in ((-k, k) if k < dm else (k,)):
                    need_s(w)
                    ACC[h] += dot(S[zslot(w)], rhs1(unpack(UB[h, zslot(w)])))
                yield
            if t > 0:
                mate_copy(PXS, PXR, px_sem, h).wait_send()
            PXS[h] = pack(fin(ACC[h, N:]))
            mate_copy(PXS, PXR, px_sem, h).start()
            need_ps()
            rhs = half(PS[t], h) - fin(ACC[h, :N])
            for k in range(dm):
                for d, c in chunks(k):
                    up_copy(h, d, k, c).wait_send()
            yield
            need_p()
            mate_copy(PXS, PXR, px_sem, h).wait_recv()
            solved = mm3(PIh[...], PIl[...], rhs - unpack(PXR[h]))
            if t > 0:
                mate_copy(SXS, SXR, sx_sem, h).wait_send()
            SXS[h] = pack(solved)
            mate_copy(SXS, SXR, sx_sem, h).start()
            RG[h, :N] = rhs1(solved)
            if H == 1:
                PO[t] = solved
            else:
                PO[t, :, h * hc : (h + 1) * hc] = solved[:, h * hc : (h + 1) * hc]
            if h == H - 1:
                out_copy(PO, par_hbm, 1, t).start()
            if t > 0:
                for k in range(dm):
                    for d, c in chunks(k):
                        dn_copy(h, d, k, c).wait_send()
            for w in range(nz):
                need_t(w)
            yield
            mate_copy(SXS, SXR, sx_sem, h).wait_recv()
            RG[h, N:] = rhs1(unpack(SXR[h]))
            g = sel(h, zslot(dm))
            SB[h, 0, dm - 1] = g
            SB[h, 1, dm - 1] = g
            for d, c in chunks(dm - 1):
                dn_copy(h, d, dm - 1, c).start()
            yield
            for k in range(dm - 2, -1, -1):
                for d in range(2):
                    SB[h, d, k] = sel(h, zslot((k + 1) * (1 if d == 0 else -1)))
                if k == dm - 2:
                    for d, c in chunks(0):
                        if not in_half(d, c):
                            dn_copy(h, d, k, c).start()
                yield
                for d, c in chunks(k + 1):
                    dn_copy(h, d, k + 1, c).wait_recv()
                    at = pl.ds(c * cr, cr)
                    SB[h, d, k, at] += RB[h, d, k + 1, at]
                    dn_copy(h, d, k, c).start()
                yield
            g = sel(h, z)
            need_d()
            for d, c in chunks(0):
                dn_copy(h, d, 0, c).wait_recv()
            down = unpack(g + RB[h, 0, 0] + RB[h, 1, 0])
            low_rows = PART[h, N - Q :] - mm3(DNh[N - Q :], DNl[N - Q :], down)
            if t < ticks - 1:
                if t > 0:
                    x_copy(h, t - 1).wait_send()
                XS[h] = pack(low_rows)
                x_copy(h, t).start()
            yield
            top_rows = PART[h, : N - Q] - mm3(DNh[: N - Q], DNl[: N - Q], down)
            for at, val in ((slice(N - Q, N), low_rows), (slice(0, N - Q), top_rows)):
                if H == 1:
                    LO[t, at] = val
                else:
                    LO[t, at, h * hc : (h + 1) * hc] = val[:, h * hc : (h + 1) * hc]
            if h == H - 1:
                out_copy(LO, leaf_hbm, 0, t).start()
            yield
        for k in range(dm):
            for d, c in chunks(k):
                dn_copy(h, d, k, c).wait_send()
        mate_copy(PXS, PXR, px_sem, h).wait_send()
        mate_copy(SXS, SXR, sx_sem, h).wait_send()
        x_copy(h, ticks - 2).wait_send()

    def background():
        for k in range(1, dm + 1):
            need_s(k)
            need_s(-k)
            yield
        need_ps()
        need_p()
        yield
        need_d()
        yield
        for w in range(nz):
            need_t(w)
            if w % 2:
                yield
        need_m()
        yield
        need_m2()
        yield
        for t in range(1, ticks):
            need_v(t)
            need_w(t)
            yield

    runs = [sweep(h) for h in range(H)]
    back = background()
    lead = 5 if H == 2 else 0
    step = 0
    live = list(range(H))
    while live:
        for h in list(live):
            if h == 1 and step < lead:
                continue
            try:
                next(runs[h])
            except StopIteration:
                live.remove(h)
        next(back, None)
        step += 1
    for _ in back:
        pass
    for t in range(ticks):
        out_copy(PO, par_hbm, 1, t).wait()
        out_copy(LO, leaf_hbm, 0, t).wait()


def local(cfg, *args):
    n_panel, n_front, ticks, H = cfg
    li, pi, up, dn, ic, ls, ps, par, cnt, rows = args
    nz = n_front // 2
    dm = nz // 2
    N, C = ls.shape[3:]
    U = up.shape[2]
    Q = ic.shape[3]
    pr = U // H
    nch = 4 // H
    wide = 2 * C // H
    v = pltpu.VMEM
    dma = pltpu.SemaphoreType.DMA
    scratch = [
        v((N, N), F32), v((N, N), F32), v((U, N), F32), v((N, U), F32), v((N, Q), F32),
        v((ticks, N, C), F32), v((ticks, N, C), F32),
        v((N, N), BF16), v((N, N), BF16), v((N, N), BF16), v((N, N), BF16),
        v((U, N), BF16), v((U, N), BF16), v((N, U), BF16), v((N, U), BF16),
        v((N, Q), BF16), v((N, Q), BF16), v((N, Q), BF16), v((N, Q), BF16), v((U, Q), BF16), v((U, Q), BF16),
        v((ticks, N, C), F32), v((ticks, U, C), F32),
        v((nz, 2 * N, U), BF16), v((nz, U, 2 * N), BF16), v((nz, U), jnp.int32),
        v((H, nz, pr, C), F32), v((H, 2, dm, pr, C), F32), v((H, 2, dm, pr, C), F32),
        v((H, N // H, C), F32), v((H, N // H, C), F32), v((H, N // H, C), F32), v((H, N // H, C), F32),
        v((H, Q // H, C), F32), v((H, ticks - 1, Q // H, C), F32),
        v((H, 2 * N, wide), F32), v((H, 2 * N, wide), BF16), v((H, N, C), F32),
        v((ticks, N, C), F32), v((ticks, N, C), F32),
        dma((7,)), dma((2, ticks)),
        dma((H, 2, dm, nch)), dma((H, 2, dm, nch)), dma((H, 2, dm, nch)), dma((H, 2, dm, nch)),
        dma((H, 2)), dma((H, 2)), dma((H,)), dma((H, ticks - 1)),
    ]
    hbm = pl.BlockSpec(memory_space=pl.ANY)
    smem = pl.BlockSpec(memory_space=pltpu.SMEM)
    return pl.pallas_call(
        functools.partial(kernel, cfg),
        out_shape=(jax.ShapeDtypeStruct(ls.shape, F32), jax.ShapeDtypeStruct(ps.shape, F32)),
        in_specs=[hbm] * 7 + [smem, smem, pl.BlockSpec(memory_space=pltpu.VMEM)],
        out_specs=(hbm, hbm),
        scratch_shapes=scratch,
        compiler_params=pltpu.CompilerParams(
            collective_id=0, has_side_effects=True, vmem_limit_bytes=62 * 1024 * 1024
        ),
        name="sweep",
    )(*args)


def solution(mesh):
    four = P("panel", "front", None, None)
    five = P("panel", "front", None, None, None)

    def step(*args):
        cfg = (mesh.shape["panel"], mesh.shape["front"], args[5].shape[2], HALVES)
        return local(cfg, *args)

    return jax.shard_map(
        step,
        mesh=mesh,
        in_specs=(four,) * 5 + (five,) * 2 + (P("panel", None), P("panel", None), P("panel", None, None)),
        out_specs=(five, five),
        check_vma=False,
    )
```

```python
import functools

import jax
import jax.numpy as jnp
from jax import lax
from jax.experimental import pallas as pl
from jax.experimental.pallas import tpu as pltpu
from jax.sharding import PartitionSpec as P

F32 = jnp.float32
BF16 = jnp.bfloat16
MESH = pl.DeviceIdType.MESH
HALVES = 2


def dot(a, b):
    return jnp.dot(a, b, preferred_element_type=F32)


def split(x):
    hi = x.astype(BF16)
    return hi, (x - hi.astype(F32)).astype(BF16)


def kernel(
    cfg,
    li_hbm, pi_hbm, up_hbm, dn_hbm, ic_hbm, ls_hbm, ps_hbm, par_ref, cnt_ref, row_ref,
    leaf_hbm, par_hbm,
    LI, PI, UP, DN, IC, LS, PS,
    LIh, LIl, PIh, PIl, UPh, UPl, DNh, DNl, ICh, ICl, Mh, Ml, M2h, M2l,
    V, W, S, T, TG, UB, RB, SB, PXS, PXR, SXS, SXR, XS, XR, ACC, RG, PART, LO, PO,
    ld_sem, st_sem, up_s, up_r, dn_s, dn_r, px_sem, sx_sem, x_s, x_r,
):
    n_panel, n_front, ticks, H = cfg
    nz = n_front // 2
    dm = nz // 2
    N, C = LS.shape[1:]
    U = UP.shape[0]
    Q = IC.shape[1]
    pr = U // H
    nch = 4 // H
    cr = pr // nch
    hc = C // 2
    panel = lax.axis_index("panel")
    front = lax.axis_index("front")
    z = front // 2
    core = lax.rem(front, 2)
    mate = front + 1 - 2 * core

    def zslot(d):
        return lax.rem(z + d + nz, nz)

    def zdev(d):
        return {"front": 2 * zslot(d) + core}

    loads = []
    for i, (src, dst) in enumerate(
        [
            (li_hbm.at[0, 0], LI), (ls_hbm.at[0, 0], LS), (up_hbm.at[0, 0], UP), (ic_hbm.at[0, 0], IC),
            (ps_hbm.at[0, 0], PS), (pi_hbm.at[0, 0], PI), (dn_hbm.at[0, 0], DN),
        ]
    ):
        loads.append(pltpu.make_async_copy(src, dst, ld_sem.at[i]))
        loads[-1].start()
    barrier = pltpu.get_barrier_semaphore()
    for who in (
        zdev(1), zdev(-1), {"front": mate},
        {"panel": lax.rem(panel + 1, n_panel)}, {"panel": lax.rem(panel + n_panel - 1, n_panel)},
    ):
        pl.semaphore_signal(barrier, inc=1, device_id=who, device_id_type=MESH)

    def low(shape):
        return lax.broadcasted_iota(jnp.int32, shape, 1) < hc

    def swap(x):
        return pltpu.roll(x, hc, 1)

    def half(x, h):
        if H == 1:
            return x
        return jnp.where(low(x.shape), x, swap(x)) if h == 0 else jnp.where(low(x.shape), swap(x), x)

    def pack(x):
        if H == 1:
            return x
        m = x.shape[0] // 2
        return jnp.where(low((m, C)), x[:m], x[m:])

    def unpack(p):
        if H == 1:
            return p
        m, s = low(p.shape), swap(p)
        return jnp.concatenate([jnp.where(m, p, s), jnp.where(m, s, p)], axis=0)

    def rhs1(x):
        if H == 1:
            return jnp.concatenate(split(x), axis=1)
        hi = x.astype(BF16).astype(F32)
        return jnp.where(low(x.shape), hi, x - hi).astype(BF16)

    def rhs2(x):
        if H == 1:
            return x.astype(BF16)
        return jnp.where(low(x.shape), x, 0.0).astype(BF16)

    def fin(o):
        if H == 1:
            return o[:, :C] + o[:, C:]
        return o + swap(o)

    def mm3(ah, al, x):
        if H == 1:
            return fin(dot(ah, rhs1(x))) + dot(al, rhs2(x))
        return fin(dot(ah, rhs1(x)) + dot(al, rhs2(x)))

    def mm3_full(ah, al, x):
        xh, xl = split(x)
        o = dot(ah, jnp.concatenate([xh, xl], axis=1))
        return o[:, :C] + o[:, C:] + dot(al, xh)

    def mmm(ah, al, bh, bl):
        return dot(ah, bh) + dot(ah, bl) + dot(al, bh)

    done = set()

    def once(key, fn):
        if key not in done:
            done.add(key)
            fn()

    def load(i, full, hi, lo):
        def go():
            loads[i].wait()
            h, l = split(full[...])
            hi[...] = h
            lo[...] = l
        once(("load", i), go)

    def need_l():
        load(0, LI, LIh, LIl)

    def need_ls():
        once("ls", lambda: loads[1].wait())

    def need_u():
        load(2, UP, UPh, UPl)

    def need_ps():
        once("ps", lambda: loads[4].wait())

    def need_p():
        load(5, PI, PIh, PIl)

    def need_d():
        load(6, DN, DNh, DNl)

    def need_v(t):
        def go():
            need_l()
            need_ls()
            V[t] = mm3_full(LIh[...], LIl[...], LS[t])
        once(("v", t), go)

    def need_w(t):
        def go():
            need_v(t)
            need_u()
            W[t] = mm3_full(UPh[...], UPl[...], V[t])
        once(("w", t), go)

    def need_m():
        def go():
            load(3, IC, ICh, ICl)
            need_l()
            h, l = split(mmm(LIh[...], LIl[...], ICh[...], ICl[...]))
            Mh[...] = h
            Ml[...] = l
        once("m", go)

    def need_m2():
        def go():
            need_m()
            need_u()
            h, l = split(mmm(UPh[...], UPl[...], Mh[...], Ml[...]))
            M2h[...] = h
            M2l[...] = l
        once("m2", go)

    def need_tg():
        def go():
            k = lax.broadcasted_iota(jnp.int32, (1, U), 1)
            for w in range(nz):
                leaf = 2 * w + core
                rows = row_ref[0, pl.ds(leaf, 1), :]
                par = jnp.full((1, U), par_ref[0, leaf], jnp.int32)
                cnt = jnp.full((1, U), cnt_ref[0, leaf], jnp.int32)
                there = jnp.where(par == front, rows, jnp.where(par == mate, rows + N, -1))
                TG[pl.ds(w, 1), :] = jnp.where(k < cnt, there, -1)
        once("tg", go)

    def need_s(d):
        def go():
            need_tg()
            w = zslot(d)
            tgt = TG[pl.ds(w, 1), :]
            i = lax.broadcasted_iota(jnp.int32, (2 * N, U), 0)
            S[w] = jnp.where(i == tgt, 1.0, 0.0).astype(BF16)
        once(("s", d % nz), go)

    def need_t(w):
        def go():
            need_tg()
            col = jnp.transpose(TG[...])[:, w : w + 1]
            i = lax.broadcasted_iota(jnp.int32, (U, 2 * N), 1)
            T[w] = jnp.where(i == col, 1.0, 0.0).astype(BF16)
        once(("t", w), go)

    def in_half(d, c):
        return c < nch // 2 if d == 0 else c >= nch // 2

    def up_copy(h, d, k, c):
        sgn = 1 if d == 0 else -1
        ref = UB.at[h, zslot(-sgn * k), pl.ds(c * cr, cr)]
        return pltpu.make_async_remote_copy(
            ref, ref, up_s.at[h, d, k, c], up_r.at[h, d, k, c], device_id=zdev(sgn), device_id_type=MESH
        )

    def up_arrival(h, d, k, c):
        sgn = 1 if d == 0 else -1
        ref = UB.at[h, zslot(-sgn * (k + 1)), pl.ds(c * cr, cr)]
        return pltpu.make_async_remote_copy(
            ref, ref, up_s.at[h, d, k, c], up_r.at[h, d, k, c], device_id=zdev(sgn), device_id_type=MESH
        )

    def dn_copy(h, d, k, c):
        sgn = 1 if d == 0 else -1
        at = pl.ds(c * cr, cr)
        return pltpu.make_async_remote_copy(
            SB.at[h, d, k, at], RB.at[h, d, k, at], dn_s.at[h, d, k, c], dn_r.at[h, d, k, c],
            device_id=zdev(sgn), device_id_type=MESH,
        )

    def mate_copy(src, dst, sem, h):
        return pltpu.make_async_remote_copy(
            src.at[h], dst.at[h], sem.at[h, 0], sem.at[h, 1], device_id={"front": mate}, device_id_type=MESH
        )

    def x_copy(h, t):
        return pltpu.make_async_remote_copy(
            XS.at[h], XR.at[h, t], x_s.at[h], x_r.at[h, t],
            device_id={"panel": lax.rem(panel + 1, n_panel)}, device_id_type=MESH,
        )

    def chunks(k):
        for c in range(nch):
            for d in range(2):
                if k < dm - 1 or in_half(d, c):
                    yield d, c

    def out_copy(src, dst, i, t):
        return pltpu.make_async_copy(src.at[t], dst.at[0, 0, t], st_sem.at[i, t])

    def sel(h, w):
        return pack(fin(dot(T[w], RG[h])))

    def sweep(h):
        for t in range(ticks):
            if t == 0:
                need_w(0)
                u = half(W[0], h)
            else:
                need_m2()
                need_w(t)
                x_copy(h, t - 1).wait_recv()
                x = jnp.where(panel > 0, unpack(XR[h, t - 1]), 0.0)
                u = half(W[t], h) + mm3(M2h[...], M2l[...], x)
            UB[h, z] = pack(u)
            if t == 0:
                once("barrier", lambda: pl.semaphore_wait(barrier, 5))
            for d, c in chunks(0):
                up_copy(h, d, 0, c).start()
            yield
            need_s(0)
            ACC[h] = dot(S[z], rhs1(u))
            if t == 0:
                need_v(0)
                PART[h] = half(V[0], h)
            else:
                need_m()
                need_v(t)
                PART[h] = half(V[t], h) + mm3(Mh[...], Ml[...], x)
            yield
            for k in range(1, dm + 1):
                for d, c in chunks(k - 1):
                    up_arrival(h, d, k - 1, c).wait_recv()
                    if k < dm and (k < dm - 1 or in_half(d, c)):
                        up_copy(h, d, k, c).start()
                yield
                for w in ((-k, k) if k < dm else (k,)):
                    need_s(w)
                    ACC[h] += dot(S[zslot(w)], rhs1(unpack(UB[h, zslot(w)])))
                yield
            if t > 0:
                mate_copy(PXS, PXR, px_sem, h).wait_send()
            PXS[h] = pack(fin(ACC[h, N:]))
            mate_copy(PXS, PXR, px_sem, h).start()
            need_ps()
            rhs = half(PS[t], h) - fin(ACC[h, :N])
            for k in range(dm):
                for d, c in chunks(k):
                    up_copy(h, d, k, c).wait_send()
            yield
            need_p()
            mate_copy(PXS, PXR, px_sem, h).wait_recv()
            solved = mm3(PIh[...], PIl[...], rhs - unpack(PXR[h]))
            if t > 0:
                mate_copy(SXS, SXR, sx_sem, h).wait_send()
            SXS[h] = pack(solved)
            mate_copy(SXS, SXR, sx_sem, h).start()
            RG[h, :N] = rhs1(solved)
            if H == 1:
                PO[t] = solved
            else:
                PO[t, :, h * hc : (h + 1) * hc] = solved[:, h * hc : (h + 1) * hc]
            if h == H - 1:
                out_copy(PO, par_hbm, 1, t).start()
            if t > 0:
                for k in range(dm):
                    for d, c in chunks(k):
                        dn_copy(h, d, k, c).wait_send()
            for w in range(nz):
                need_t(w)
            yield
            mate_copy(SXS, SXR, sx_sem, h).wait_recv()
            RG[h, N:] = rhs1(unpack(SXR[h]))
            g = sel(h, zslot(dm))
            SB[h, 0, dm - 1] = g
            SB[h, 1, dm - 1] = g
            for d, c in chunks(dm - 1):
                dn_copy(h, d, dm - 1, c).start()
            yield
            for k in range(dm - 2, -1, -1):
                for d in range(2):
                    SB[h, d, k] = sel(h, zslot((k + 1) * (1 if d == 0 else -1)))
                if k == dm - 2:
                    for d, c in chunks(0):
                        if not in_half(d, c):
                            dn_copy(h, d, k, c).start()
                yield
                for d, c in chunks(k + 1):
                    dn_copy(h, d, k + 1, c).wait_recv()
                    at = pl.ds(c * cr, cr)
                    SB[h, d, k, at] += RB[h, d, k + 1, at]
                    dn_copy(h, d, k, c).start()
                yield
            g = sel(h, z)
            need_d()
            for d, c in chunks(0):
                dn_copy(h, d, 0, c).wait_recv()
            down = unpack(g + RB[h, 0, 0] + RB[h, 1, 0])
            low_rows = PART[h, N - Q :] - mm3(DNh[N - Q :], DNl[N - Q :], down)
            if t < ticks - 1:
                if t > 0:
                    x_copy(h, t - 1).wait_send()
                XS[h] = pack(low_rows)
                x_copy(h, t).start()
            yield
            top_rows = PART[h, : N - Q] - mm3(DNh[: N - Q], DNl[: N - Q], down)
            for at, val in ((slice(N - Q, N), low_rows), (slice(0, N - Q), top_rows)):
                if H == 1:
                    LO[t, at] = val
                else:
                    LO[t, at, h * hc : (h + 1) * hc] = val[:, h * hc : (h + 1) * hc]
            if h == H - 1:
                out_copy(LO, leaf_hbm, 0, t).start()
            yield
        for k in range(dm):
            for d, c in chunks(k):
                dn_copy(h, d, k, c).wait_send()
        mate_copy(PXS, PXR, px_sem, h).wait_send()
        mate_copy(SXS, SXR, sx_sem, h).wait_send()
        x_copy(h, ticks - 2).wait_send()

    def background():
        for k in range(1, dm + 1):
            need_s(k)
            need_s(-k)
            yield
        need_ps()
        need_p()
        yield
        need_d()
        yield
        for w in range(nz):
            need_t(w)
            if w % 2:
                yield
        need_m()
        yield
        need_m2()
        yield
        for t in range(1, ticks):
            need_v(t)
            need_w(t)
            yield

    runs = [sweep(h) for h in range(H)]
    back = background()
    lead = 5 if H == 2 else 0
    step = 0
    live = list(range(H))
    while live:
        for h in list(live):
            if h == 1 and step < lead:
                continue
            try:
                next(runs[h])
            except StopIteration:
                live.remove(h)
        next(back, None)
        step += 1
    for _ in back:
        pass
    for t in range(ticks):
        out_copy(PO, par_hbm, 1, t).wait()
        out_copy(LO, leaf_hbm, 0, t).wait()


def local(cfg, *args):
    n_panel, n_front, ticks, H = cfg
    li, pi, up, dn, ic, ls, ps, par, cnt, rows = args
    nz = n_front // 2
    dm = nz // 2
    N, C = ls.shape[3:]
    U = up.shape[2]
    Q = ic.shape[3]
    pr = U // H
    nch = 4 // H
    wide = 2 * C // H
    v = pltpu.VMEM
    dma = pltpu.SemaphoreType.DMA
    scratch = [
        v((N, N), F32), v((N, N), F32), v((U, N), F32), v((N, U), F32), v((N, Q), F32),
        v((ticks, N, C), F32), v((ticks, N, C), F32),
        v((N, N), BF16), v((N, N), BF16), v((N, N), BF16), v((N, N), BF16),
        v((U, N), BF16), v((U, N), BF16), v((N, U), BF16), v((N, U), BF16),
        v((N, Q), BF16), v((N, Q), BF16), v((N, Q), BF16), v((N, Q), BF16), v((U, Q), BF16), v((U, Q), BF16),
        v((ticks, N, C), F32), v((ticks, U, C), F32),
        v((nz, 2 * N, U), BF16), v((nz, U, 2 * N), BF16), v((nz, U), jnp.int32),
        v((H, nz, pr, C), F32), v((H, 2, dm, pr, C), F32), v((H, 2, dm, pr, C), F32),
        v((H, N // H, C), F32), v((H, N // H, C), F32), v((H, N // H, C), F32), v((H, N // H, C), F32),
        v((H, Q // H, C), F32), v((H, ticks - 1, Q // H, C), F32),
        v((H, 2 * N, wide), F32), v((H, 2 * N, wide), BF16), v((H, N, C), F32),
        v((ticks, N, C), F32), v((ticks, N, C), F32),
        dma((7,)), dma((2, ticks)),
        dma((H, 2, dm, nch)), dma((H, 2, dm, nch)), dma((H, 2, dm, nch)), dma((H, 2, dm, nch)),
        dma((H, 2)), dma((H, 2)), dma((H,)), dma((H, ticks - 1)),
    ]
    hbm = pl.BlockSpec(memory_space=pl.ANY)
    smem = pl.BlockSpec(memory_space=pltpu.SMEM)
    return pl.pallas_call(
        functools.partial(kernel, cfg),
        out_shape=(jax.ShapeDtypeStruct(ls.shape, F32), jax.ShapeDtypeStruct(ps.shape, F32)),
        in_specs=[hbm] * 7 + [smem, smem, pl.BlockSpec(memory_space=pltpu.VMEM)],
        out_specs=(hbm, hbm),
        scratch_shapes=scratch,
        compiler_params=pltpu.CompilerParams(
            collective_id=0, has_side_effects=True, vmem_limit_bytes=62 * 1024 * 1024
        ),
        name="sweep",
    )(*args)


def solution(mesh):
    four = P("panel", "front", None, None)
    five = P("panel", "front", None, None, None)

    def step(*args):
        cfg = (mesh.shape["panel"], mesh.shape["front"], args[5].shape[2], HALVES)
        return local(cfg, *args)

    return jax.shard_map(
        step,
        mesh=mesh,
        in_specs=(four,) * 5 + (five,) * 2 + (P("panel", None), P("panel", None), P("panel", None, None)),
        out_specs=(five, five),
        check_vma=False,
    )
```

```python
import functools

import jax
import jax.numpy as jnp
from jax import lax
from jax.experimental import pallas as pl
from jax.experimental.pallas import tpu as pltpu
from jax.sharding import PartitionSpec as P

F32 = jnp.float32
BF16 = jnp.bfloat16
MESH = pl.DeviceIdType.MESH
HALF = 7.1
PERIOD = 4 * HALF


def dot(a, b):
    return jnp.dot(a, b, preferred_element_type=F32)


def split(x):
    hi = x.astype(BF16)
    return hi, (x - hi.astype(F32)).astype(BF16)


def kernel(
    cfg,
    li_hbm, pi_hbm, up_hbm, dn_hbm, ic_hbm, ls_hbm, ps_hbm, par_ref, cnt_ref, row_ref,
    leaf_hbm, par_hbm,
    LI, PI, UP, DN, IC, LS, PS,
    LIh, LIl, PIh, PIl, UPh, UPl, DNh, DNl, ICh, ICl, Mh, Ml, M2h, M2l,
    V, W, S, T, TG, UB, RB, SB, PXS, PXR, SXS, SXR, XS, XR, ACC, RG, PART, LO, PO,
    ld_sem, st_sem, up_s, up_r, dn_s, dn_r, px_sem, sx_sem, x_s, x_r,
):
    n_panel, n_front, ticks = cfg
    nz = n_front // 2
    dm = nz // 2
    N, C = LS.shape[1:]
    U = UP.shape[0]
    Q = IC.shape[1]
    pr = U // 2
    cr = pr // 2
    hc = C // 2
    panel = lax.axis_index("panel")
    front = lax.axis_index("front")
    z = front // 2
    core = lax.rem(front, 2)
    mate = front + 1 - 2 * core

    def zslot(d):
        return lax.rem(z + d + nz, nz)

    def zdev(d):
        return {"front": 2 * zslot(d) + core}

    ins = [(li_hbm.at[0, 0], LI), (ls_hbm.at[0, 0, 0], LS.at[0]), (up_hbm.at[0, 0], UP), (ps_hbm.at[0, 0], PS)]
    ins += [(pi_hbm.at[0, 0], PI), (ic_hbm.at[0, 0], IC), (ls_hbm.at[0, 0, 1:], LS.at[1:]), (dn_hbm.at[0, 0], DN)]
    loads = [pltpu.make_async_copy(src, dst, ld_sem.at[i]) for i, (src, dst) in enumerate(ins)]
    for c in loads:
        c.start()
    barrier = pltpu.get_barrier_semaphore()
    for who in (
        zdev(1), zdev(-1), {"front": mate},
        {"panel": lax.rem(panel + 1, n_panel)}, {"panel": lax.rem(panel + n_panel - 1, n_panel)},
    ):
        pl.semaphore_signal(barrier, inc=1, device_id=who, device_id_type=MESH)

    def low(shape):
        return lax.broadcasted_iota(jnp.int32, shape, 1) < hc

    def swap(x):
        return pltpu.roll(x, hc, 1)

    def half(x, h):
        return jnp.where(low(x.shape), x, swap(x)) if h == 0 else jnp.where(low(x.shape), swap(x), x)

    def pack(x):
        m = x.shape[0] // 2
        return jnp.where(low((m, C)), x[:m], x[m:])

    def unpack(p):
        m, s = low(p.shape), swap(p)
        return jnp.concatenate([jnp.where(m, p, s), jnp.where(m, s, p)], axis=0)

    def hilo(x):
        hi = x.astype(BF16).astype(F32)
        return jnp.where(low(x.shape), hi, x - hi)

    def fin(o):
        return o + swap(o)

    def mm3(ah, al, x):
        return fin(dot(ah, hilo(x).astype(BF16)) + dot(al, jnp.where(low(x.shape), x, 0.0).astype(BF16)))

    def mm3_full(ah, al, x):
        xh, xl = split(x)
        o = dot(ah, jnp.concatenate([xh, xl], axis=1))
        return o[:, :C] + o[:, C:] + dot(al, xh)

    def mmm(ah, al, bh, bl):
        return dot(ah, bh) + dot(ah, bl) + dot(al, bh)

    def store2(x, hi, lo):
        h, l = split(x)
        hi[...] = h
        lo[...] = l

    def in_half(d, c):
        return c == d

    def chunks(k, c):
        return [d for d in range(2) if k < dm - 1 or in_half(d, c)]

    def up_copy(h, d, k, c, back=0):
        sgn = 1 if d == 0 else -1
        ref = UB.at[h, zslot(-sgn * (k + back)), pl.ds(c * cr, cr)]
        return pltpu.make_async_remote_copy(
            ref, ref, up_s.at[h, d, k, c], up_r.at[h, d, k, c], device_id=zdev(sgn), device_id_type=MESH
        )

    def dn_copy(h, d, k, c):
        at = pl.ds(c * cr, cr)
        return pltpu.make_async_remote_copy(
            SB.at[h, d, k, at], RB.at[h, d, k, at], dn_s.at[h, d, k, c], dn_r.at[h, d, k, c],
            device_id=zdev(1 if d == 0 else -1), device_id_type=MESH,
        )

    def mate_copy(src, dst, sem, h):
        return pltpu.make_async_remote_copy(
            src.at[h], dst.at[h], sem.at[h, 0], sem.at[h, 1], device_id={"front": mate}, device_id_type=MESH
        )

    def x_copy(h, t):
        return pltpu.make_async_remote_copy(
            XS.at[h], XR.at[h, t], x_s.at[h], x_r.at[h, t],
            device_id={"panel": lax.rem(panel + 1, n_panel)}, device_id_type=MESH,
        )

    def all_sends(copy, h):
        for k in range(dm):
            for c in range(2):
                for d in chunks(k, c):
                    copy(h, d, k, c).wait_send()

    def out_copy(src, dst, i, t):
        return pltpu.make_async_copy(src.at[t], dst.at[0, 0, t], st_sem.at[i, t])

    def share(h, k):
        w = zslot(k)
        par = jnp.full((1, C), par_ref[0, 2 * w + core], jnp.int32)
        r = hilo(unpack(UB[h, w]))
        both = [jnp.where(par == who, r, 0.0).astype(BF16) for who in (front, mate)]
        return dot(S[w], jnp.concatenate(both, axis=1))

    def sel(h, k):
        w = zslot(k)
        par = par_ref[0, 2 * w + core]
        which = jnp.where(par == front, 0, jnp.where(par == mate, 1, 2))
        return pack(fin(dot(T[w], RG[h, which])))

    def start(h):
        for c in range(2):
            for d in range(2):
                up_copy(h, d, 0, c).start()

    def relay(h, k, c):
        for d in chunks(k - 1, c):
            up_copy(h, d, k - 1, c, back=1).wait_recv()
            if k < dm and (k < dm - 1 or in_half(d, c)):
                up_copy(h, d, k, c).start()

    def gather(h, k):
        if k == 0:
            ACC[h] = share(h, 0)
        elif k < dm:
            ACC[h] += share(h, -k) + share(h, k)
        else:
            ACC[h] += share(h, k)

    def arrived(h, t):
        return jnp.where(panel > 0, unpack(XR[h, t - 1]), 0.0)

    def partial(h, t):
        @pl.when(t == 0)
        def _():
            PART[h] = half(V[0], h)

        @pl.when(t > 0)
        def _():
            PART[h] = half(V[t], h) + mm3(Mh[...], Ml[...], arrived(h, t))

    def give(h, t):
        @pl.when(t > 0)
        def _():
            mate_copy(PXS, PXR, px_sem, h).wait_send()
        PXS[h] = pack(fin(ACC[h, :, C:]))
        mate_copy(PXS, PXR, px_sem, h).start()

    def solve(h, t):
        rhs = half(PS[t], h) - fin(ACC[h, :, :C])
        mate_copy(PXS, PXR, px_sem, h).wait_recv()
        solved = mm3(PIh[...], PIl[...], rhs - unpack(PXR[h]))

        @pl.when(t > 0)
        def _():
            mate_copy(SXS, SXR, sx_sem, h).wait_send()
        SXS[h] = pack(solved)
        mate_copy(SXS, SXR, sx_sem, h).start()
        RG[h, 0] = hilo(solved).astype(BF16)
        PO[t, :, h * hc : (h + 1) * hc] = solved[:, h * hc : (h + 1) * hc]
        if h == 1:
            out_copy(PO, par_hbm, 1, t).start()

    def descend(h, t):
        all_sends(up_copy, h)

        @pl.when(t > 0)
        def _():
            all_sends(dn_copy, h)
        mate_copy(SXS, SXR, sx_sem, h).wait_recv()
        RG[h, 1] = hilo(unpack(SXR[h])).astype(BF16)
        g = sel(h, dm)
        for d in range(2):
            at = pl.ds(d * cr, cr)
            SB[h, d, dm - 1, at] = g[d * cr : (d + 1) * cr]
            dn_copy(h, d, dm - 1, d).start()

    def own(h, k):
        for d in range(2):
            SB[h, d, k] = sel(h, (k + 1) * (1 if d == 0 else -1))
        if k == dm - 2:
            for d in range(2):
                dn_copy(h, d, k, 1 - d).start()

    def hop(h, k, c):
        at = pl.ds(c * cr, cr)
        for d in chunks(k + 1, c):
            dn_copy(h, d, k + 1, c).wait_recv()
            SB[h, d, k, at] += RB[h, d, k + 1, at]
            dn_copy(h, d, k, c).start()

    def leaf(h, t, last):
        g = sel(h, 0)
        for c in range(2):
            for d in range(2):
                dn_copy(h, d, 0, c).wait_recv()
        down = unpack(g + RB[h, 0, 0] + RB[h, 1, 0])
        rest = PART[h, N - Q :] - mm3(DNh[N - Q :], DNl[N - Q :], down)

        def send():
            @pl.when(t > 0)
            def _():
                x_copy(h, t - 1).wait_send()
            XS[h] = pack(rest)
            x_copy(h, t).start()
        if last is None:
            pl.when(t < ticks - 1)(send)
        elif not last:
            send()
        top = PART[h, : N - Q] - mm3(DNh[: N - Q], DNl[: N - Q], down)
        LO[t, : N - Q, h * hc : (h + 1) * hc] = top[:, h * hc : (h + 1) * hc]
        LO[t, N - Q :, h * hc : (h + 1) * hc] = rest[:, h * hc : (h + 1) * hc]
        if h == 1:
            out_copy(LO, leaf_hbm, 0, t).start()

    def update(h, t):
        x_copy(h, t - 1).wait_recv()
        UB[h, z] = pack(half(W[t], h) + mm3(M2h[...], M2l[...], arrived(h, t)))

    def targets():
        k = lax.broadcasted_iota(jnp.int32, (1, U), 1)
        for w in range(nz):
            rows = row_ref[0, pl.ds(2 * w + core, 1), :]
            cnt = jnp.full((1, U), cnt_ref[0, 2 * w + core], jnp.int32)
            TG[pl.ds(w, 1), :] = jnp.where(k < cnt, rows, -1)
        RG[0, 2] = jnp.zeros((N, C), BF16)
        RG[1, 2] = jnp.zeros((N, C), BF16)

    def make_s(k):
        w = zslot(k)
        i = lax.broadcasted_iota(jnp.int32, (N, U), 0)
        S[w] = jnp.where(i == TG[pl.ds(w, 1), :], 1.0, 0.0).astype(BF16)

    def make_t(w):
        col = jnp.transpose(TG[...])[:, w : w + 1]
        i = lax.broadcasted_iota(jnp.int32, (U, N), 1)
        T[w] = jnp.where(i == col, 1.0, 0.0).astype(BF16)

    def ready(i, full, hi, lo):
        loads[i].wait()
        store2(full[...], hi, lo)

    def static(t):
        V[t] = mm3_full(LIh[...], LIl[...], LS[t])
        W[t] = mm3_full(UPh[...], UPl[...], V[t])

    loads[0].wait()
    store2(LI[...], LIh, LIl)
    loads[1].wait()
    V[0] = mm3_full(LIh[...], LIl[...], LS[0])
    ready(2, UP, UPh, UPl)
    W[0] = mm3_full(UPh[...], UPl[...], V[0])
    for h in range(2):
        UB[h, z] = pack(half(W[0], h))
    pl.semaphore_wait(barrier, 5)

    def tick(t, carry):
        steps = []

        def at(when, fn, *args):
            steps.append((when, len(steps), functools.partial(fn, *args)))

        def only(when, cond, fn, *args):
            def run():
                fn(*args)

            def go():
                pl.when(cond)(run)
            steps.append((when, len(steps), go))

        for h in range(2):
            b = HALF * h
            at(b, start, h)
            at(b + 0.05, gather, h, 0)
            at(b + 0.5, partial, h, t)
            for k in range(1, dm + 1):
                for c in range(2):
                    at(b + 1.4 + 2 * (k - 1) + (c + 1 if k < dm else 0.9 + 0.1 * c), relay, h, k, c)
                at(b + 1.4 + 2 * k - (0 if k < dm else 0.9) + 0.05, gather, h, k)
            at(b + 1.4 + 2 * dm, give, h, t)
            at(b + 10.5, solve, h, t)
            at(b + 12.4, descend, h, t)
            b += 12.5
            at(b + 0.1, own, h, dm - 2)
            at(b + 1.0, own, h, 1)
            for c in range(2):
                at(b + 2.3 + 0.1 * c, hop, h, dm - 2, c)
                at(b + 3.4 + c, hop, h, 1, c)
                at(b + 5.4 + c, hop, h, 0, c)
            at(b + 2.5, own, h, 0)
        at(21.3, leaf, 0, t, None)
        only(26.0, t < ticks - 1, update, 0, t + 1)
        only(0.5, t > 0, leaf, 1, t - 1, False)
        only(HALF - 0.1, t > 0, update, 1, t)
        one = t == 0
        only(0.01, one, targets)
        only(0.02, one, make_s, 0)
        for k in range(1, dm):
            only(0.3 + 2 * k, one, make_s, k)
            only(0.3 + 2 * k, one, make_s, -k)
        only(0.3 + 2 * dm, one, make_s, dm)
        only(0.7, one, lambda: (loads[3].wait(), ready(4, PI, PIh, PIl)))
        for w in range(nz):
            only(3.5 + w // 2, one, make_t, w)
        only(4.0, one, lambda: (ready(5, IC, ICh, ICl), loads[6].wait()))
        only(4.1, one, lambda: store2(mmm(LIh[...], LIl[...], ICh[...], ICl[...]), Mh, Ml))
        only(6.9, one, static, 1)
        only(9.0, one, lambda: ready(7, DN, DNh, DNl))
        only(17.0, one, lambda: store2(mmm(UPh[...], UPl[...], Mh[...], Ml[...]), M2h, M2l))
        only(24.0, one, static, 2)
        for _, _, fn in sorted(steps, key=lambda s: s[:2]):
            fn()
        return carry

    lax.fori_loop(0, ticks, tick, 0)
    leaf(1, ticks - 1, True)
    for h in range(2):
        all_sends(dn_copy, h)
        mate_copy(PXS, PXR, px_sem, h).wait_send()
        mate_copy(SXS, SXR, sx_sem, h).wait_send()
        x_copy(h, ticks - 2).wait_send()
    for t in range(ticks):
        out_copy(PO, par_hbm, 1, t).wait()
        out_copy(LO, leaf_hbm, 0, t).wait()


def local(cfg, *args):
    n_panel, n_front, ticks = cfg
    li, pi, up, dn, ic, ls, ps, par, cnt, rows = args
    nz = n_front // 2
    dm = nz // 2
    N, C = ls.shape[3:]
    U = up.shape[2]
    Q = ic.shape[3]
    pr = U // 2
    v = pltpu.VMEM
    dma = pltpu.SemaphoreType.DMA
    scratch = [
        v((N, N), F32), v((N, N), F32), v((U, N), F32), v((N, U), F32), v((N, Q), F32),
        v((ticks, N, C), F32), v((ticks, N, C), F32),
        v((N, N), BF16), v((N, N), BF16), v((N, N), BF16), v((N, N), BF16),
        v((U, N), BF16), v((U, N), BF16), v((N, U), BF16), v((N, U), BF16),
        v((N, Q), BF16), v((N, Q), BF16), v((N, Q), BF16), v((N, Q), BF16), v((U, Q), BF16), v((U, Q), BF16),
        v((ticks, N, C), F32), v((ticks, U, C), F32),
        v((nz, N, U), BF16), v((nz, U, N), BF16), v((nz, U), jnp.int32),
        v((2, nz, pr, C), F32), v((2, 2, dm, pr, C), F32), v((2, 2, dm, pr, C), F32),
        v((2, N // 2, C), F32), v((2, N // 2, C), F32), v((2, N // 2, C), F32), v((2, N // 2, C), F32),
        v((2, Q // 2, C), F32), v((2, ticks - 1, Q // 2, C), F32),
        v((2, N, 2 * C), F32), v((2, 3, N, C), BF16), v((2, N, C), F32),
        v((ticks, N, C), F32), v((ticks, N, C), F32),
        dma((8,)), dma((2, ticks)),
        dma((2, 2, dm, 2)), dma((2, 2, dm, 2)), dma((2, 2, dm, 2)), dma((2, 2, dm, 2)),
        dma((2, 2)), dma((2, 2)), dma((2,)), dma((2, ticks - 1)),
    ]
    hbm = pl.BlockSpec(memory_space=pl.ANY)
    smem = pl.BlockSpec(memory_space=pltpu.SMEM)
    return pl.pallas_call(
        functools.partial(kernel, cfg),
        out_shape=(jax.ShapeDtypeStruct(ls.shape, F32), jax.ShapeDtypeStruct(ps.shape, F32)),
        in_specs=[hbm] * 7 + [smem, smem, pl.BlockSpec(memory_space=pltpu.VMEM)],
        out_specs=(hbm, hbm),
        scratch_shapes=scratch,
        compiler_params=pltpu.CompilerParams(
            collective_id=0, has_side_effects=True, vmem_limit_bytes=62 * 1024 * 1024
        ),
        name="sweep",
    )(*args)


def solution(mesh):
    four = P("panel", "front", None, None)
    five = P("panel", "front", None, None, None)

    def step(*args):
        cfg = (mesh.shape["panel"], mesh.shape["front"], args[5].shape[2])
        return local(cfg, *args)

    return jax.shard_map(
        step,
        mesh=mesh,
        in_specs=(four,) * 5 + (five,) * 2 + (P("panel", None), P("panel", None), P("panel", None, None)),
        out_specs=(five, five),
        check_vma=False,
    )
```

```python
import functools

import jax
import jax.numpy as jnp
from jax import lax
from jax.experimental import pallas as pl
from jax.experimental.pallas import tpu as pltpu
from jax.sharding import PartitionSpec as P

F32 = jnp.float32
BF16 = jnp.bfloat16
MESH = pl.DeviceIdType.MESH
ORDER = (
    0, 80, 62, 69, 65, 63, 1, 59, 3, 4, 84, 2, 6, 61, 64, 7, 79, 31, 5, 66, 68, 32, 77, 9, 60, 67, 10, 8, 34, 71, 11,
    35, 72, 76, 74, 12, 13, 73, 75, 70, 14, 37, 15, 38, 36, 16, 78, 40, 39, 41, 17, 19, 18, 43, 42, 44, 45, 22, 46,
    85, 23, 47, 24, 48, 25, 52, 49, 21, 20, 53, 26, 50, 54, 51, 27, 81, 55, 56, 33, 28, 29, 83, 57, 82, 58, 30,
)


def dot(a, b):
    return jnp.dot(a, b, preferred_element_type=F32)


def split(x):
    hi = x.astype(BF16)
    return hi, (x - hi.astype(F32)).astype(BF16)


def kernel(
    cfg,
    li_hbm, pi_hbm, up_hbm, dn_hbm, ic_hbm, ls_hbm, ps_hbm, par_ref, cnt_ref, row_ref,
    leaf_hbm, par_hbm,
    LI, PI, UP, DN, IC, LS, PS,
    LIh, LIl, PIh, PIl, UPh, UPl, DNh, DNl, ICh, ICl, Mh, Ml, M2h, M2l,
    V, W, S, T, TG, UB, RB, SB, PXS, PXR, SXS, SXR, XS, XR, ACC, RG, PART, MINE, DOWN, LO, PO,
    ld_sem, st_sem, up_s, up_r, dn_s, dn_r, px_sem, sx_sem, x_s, x_r,
):
    n_panel, n_front, ticks = cfg
    nz = n_front // 2
    dm = nz // 2
    N, C = LS.shape[1:]
    U = UP.shape[0]
    Q = IC.shape[1]
    pr = U // 2
    cr = pr // 2
    hc = C // 2
    panel = lax.axis_index("panel")
    front = lax.axis_index("front")
    z = front // 2
    core = lax.rem(front, 2)
    mate = front + 1 - 2 * core

    def zslot(d):
        return lax.rem(z + d + nz, nz)

    def zdev(d):
        return {"front": 2 * zslot(d) + core}

    ins = [(li_hbm.at[0, 0], LI), (ls_hbm.at[0, 0, 0], LS.at[0]), (up_hbm.at[0, 0], UP), (ps_hbm.at[0, 0], PS)]
    ins += [(pi_hbm.at[0, 0], PI), (ic_hbm.at[0, 0], IC), (ls_hbm.at[0, 0, 1:], LS.at[1:]), (dn_hbm.at[0, 0], DN)]
    loads = [pltpu.make_async_copy(src, dst, ld_sem.at[i]) for i, (src, dst) in enumerate(ins)]
    for c in loads:
        c.start()
    barrier = pltpu.get_barrier_semaphore()
    for who in (
        zdev(1), zdev(-1), {"front": mate},
        {"panel": lax.rem(panel + 1, n_panel)}, {"panel": lax.rem(panel + n_panel - 1, n_panel)},
    ):
        pl.semaphore_signal(barrier, inc=1, device_id=who, device_id_type=MESH)

    def low(shape):
        return lax.broadcasted_iota(jnp.int32, shape, 1) < hc

    def swap(x):
        return pltpu.roll(x, hc, 1)

    def half(x, h):
        return jnp.where(low(x.shape), x, swap(x)) if h == 0 else jnp.where(low(x.shape), swap(x), x)

    def pack(x):
        m = x.shape[0] // 2
        return jnp.where(low((m, C)), x[:m], x[m:])

    def unpack(p):
        m, s = low(p.shape), swap(p)
        return jnp.concatenate([jnp.where(m, p, s), jnp.where(m, s, p)], axis=0)

    def hilo(x):
        hi = x.astype(BF16).astype(F32)
        return jnp.where(low(x.shape), hi, x - hi)

    def fin(o):
        return o + swap(o)

    def mm3(ah, al, x):
        return fin(dot(ah, hilo(x).astype(BF16)) + dot(al, jnp.where(low(x.shape), x, 0.0).astype(BF16)))

    def mm3_full(ah, al, x):
        xh, xl = split(x)
        o = dot(ah, jnp.concatenate([xh, xl], axis=1))
        return o[:, :C] + o[:, C:] + dot(al, xh)

    def mmm(ah, al, bh, bl):
        return dot(ah, bh) + dot(ah, bl) + dot(al, bh)

    def store2(x, hi, lo):
        h, l = split(x)
        hi[...] = h
        lo[...] = l

    def in_half(d, c):
        return c == d

    def chunks(k, c):
        return [d for d in range(2) if k < dm - 1 or in_half(d, c)]

    def up_copy(h, d, k, c, back=0):
        sgn = 1 if d == 0 else -1
        ref = UB.at[h, zslot(-sgn * (k + back)), pl.ds(c * cr, cr)]
        return pltpu.make_async_remote_copy(
            ref, ref, up_s.at[h, d, k, c], up_r.at[h, d, k, c], device_id=zdev(sgn), device_id_type=MESH
        )

    def dn_copy(h, d, k, c):
        at = pl.ds(c * cr, cr)
        return pltpu.make_async_remote_copy(
            SB.at[h, d, k, at], RB.at[h, d, k, at], dn_s.at[h, d, k, c], dn_r.at[h, d, k, c],
            device_id=zdev(1 if d == 0 else -1), device_id_type=MESH,
        )

    def mate_copy(src, dst, sem, h):
        return pltpu.make_async_remote_copy(
            src.at[h], dst.at[h], sem.at[h, 0], sem.at[h, 1], device_id={"front": mate}, device_id_type=MESH
        )

    def x_copy(h, t):
        return pltpu.make_async_remote_copy(
            XS.at[h], XR.at[h, t], x_s.at[h], x_r.at[h, t],
            device_id={"panel": lax.rem(panel + 1, n_panel)}, device_id_type=MESH,
        )

    def all_sends(copy, h):
        for k in range(dm):
            for c in range(2):
                for d in chunks(k, c):
                    copy(h, d, k, c).wait_send()

    def out_copy(src, dst, i, t):
        return pltpu.make_async_copy(src.at[t], dst.at[0, 0, t], st_sem.at[i, t])

    def share(h, k):
        w = zslot(k)
        par = jnp.full((1, C), par_ref[0, 2 * w + core], jnp.int32)
        r = hilo(unpack(UB[h, w]))
        both = [jnp.where(par == who, r, 0.0).astype(BF16) for who in (front, mate)]
        return dot(S[w], jnp.concatenate(both, axis=1))

    def sel(h, k):
        w = zslot(k)
        par = par_ref[0, 2 * w + core]
        which = jnp.where(par == front, 0, jnp.where(par == mate, 1, 2))
        return pack(fin(dot(T[w], RG[h, which])))

    def start(h):
        for c in range(2):
            for d in range(2):
                up_copy(h, d, 0, c).start()

    def relay(h, k, c):
        for d in chunks(k - 1, c):
            up_copy(h, d, k - 1, c, back=1).wait_recv()
            if k < dm and (k < dm - 1 or in_half(d, c)):
                up_copy(h, d, k, c).start()

    def gather(h, k):
        if k == 0:
            ACC[h] = share(h, 0)
        elif k < dm:
            ACC[h] += share(h, -k) + share(h, k)
        else:
            ACC[h] += share(h, k)

    def arrived(h, t):
        return jnp.where(panel > 0, unpack(XR[h, t - 1]), 0.0)

    def partial(h, t):
        @pl.when(t == 0)
        def _():
            PART[h] = half(V[0], h)

        @pl.when(t > 0)
        def _():
            PART[h] = half(V[t], h) + mm3(Mh[...], Ml[...], arrived(h, t))

    def give(h, t):
        @pl.when(t > 0)
        def _():
            mate_copy(PXS, PXR, px_sem, h).wait_send()
        PXS[h] = pack(fin(ACC[h, :, C:]))
        mate_copy(PXS, PXR, px_sem, h).start()

    def solve(h, t):
        rhs = half(PS[t], h) - fin(ACC[h, :, :C])
        mate_copy(PXS, PXR, px_sem, h).wait_recv()
        solved = mm3(PIh[...], PIl[...], rhs - unpack(PXR[h]))

        @pl.when(t > 0)
        def _():
            mate_copy(SXS, SXR, sx_sem, h).wait_send()
        SXS[h] = pack(solved)
        mate_copy(SXS, SXR, sx_sem, h).start()
        RG[h, 0] = hilo(solved).astype(BF16)
        PO[t, :, h * hc : (h + 1) * hc] = solved[:, h * hc : (h + 1) * hc]
        if h == 1:
            out_copy(PO, par_hbm, 1, t).start()

    def descend(h, t):
        all_sends(up_copy, h)

        @pl.when(t > 0)
        def _():
            all_sends(dn_copy, h)
        mate_copy(SXS, SXR, sx_sem, h).wait_recv()
        RG[h, 1] = hilo(unpack(SXR[h])).astype(BF16)
        g = sel(h, dm)
        for d in range(2):
            at = pl.ds(d * cr, cr)
            SB[h, d, dm - 1, at] = g[d * cr : (d + 1) * cr]
            dn_copy(h, d, dm - 1, d).start()

    def own(h, k):
        if k < 0:
            MINE[h] = sel(h, 0)
            return
        for d in range(2):
            SB[h, d, k] = sel(h, (k + 1) * (1 if d == 0 else -1))
        if k == dm - 2:
            for d in range(2):
                dn_copy(h, d, k, 1 - d).start()

    def hop(h, k, c):
        at = pl.ds(c * cr, cr)
        for d in chunks(k + 1, c):
            dn_copy(h, d, k + 1, c).wait_recv()
            SB[h, d, k, at] += RB[h, d, k + 1, at]
            dn_copy(h, d, k, c).start()

    def leaf(h, t, last):
        for c in range(2):
            for d in range(2):
                dn_copy(h, d, 0, c).wait_recv()
        down = unpack(MINE[h] + RB[h, 0, 0] + RB[h, 1, 0])
        DOWN[h] = down
        rest = PART[h, N - Q :] - mm3(DNh[N - Q :], DNl[N - Q :], down)

        def send():
            @pl.when(t > 0)
            def _():
                x_copy(h, t - 1).wait_send()
            XS[h] = pack(rest)
            x_copy(h, t).start()
        if last is None:
            pl.when(t < ticks - 1)(send)
        elif not last:
            send()
        LO[t, N - Q :, h * hc : (h + 1) * hc] = rest[:, h * hc : (h + 1) * hc]

    def top(h, t):
        rest = PART[h, : N - Q] - mm3(DNh[: N - Q], DNl[: N - Q], DOWN[h])
        LO[t, : N - Q, h * hc : (h + 1) * hc] = rest[:, h * hc : (h + 1) * hc]
        if h == 1:
            out_copy(LO, leaf_hbm, 0, t).start()

    def update(h, t):
        x_copy(h, t - 1).wait_recv()
        UB[h, z] = pack(half(W[t], h) + mm3(M2h[...], M2l[...], arrived(h, t)))

    def targets():
        k = lax.broadcasted_iota(jnp.int32, (1, U), 1)
        for w in range(nz):
            rows = row_ref[0, pl.ds(2 * w + core, 1), :]
            cnt = jnp.full((1, U), cnt_ref[0, 2 * w + core], jnp.int32)
            TG[pl.ds(w, 1), :] = jnp.where(k < cnt, rows, -1)
        RG[0, 2] = jnp.zeros((N, C), BF16)
        RG[1, 2] = jnp.zeros((N, C), BF16)

    def make_s(k):
        w = zslot(k)
        i = lax.broadcasted_iota(jnp.int32, (N, U), 0)
        S[w] = jnp.where(i == TG[pl.ds(w, 1), :], 1.0, 0.0).astype(BF16)

    def make_t(w):
        col = jnp.transpose(TG[...])[:, w : w + 1]
        i = lax.broadcasted_iota(jnp.int32, (U, N), 1)
        T[w] = jnp.where(i == col, 1.0, 0.0).astype(BF16)

    def ready(i, full, hi, lo):
        loads[i].wait()
        store2(full[...], hi, lo)

    def static(t):
        V[t] = mm3_full(LIh[...], LIl[...], LS[t])
        W[t] = mm3_full(UPh[...], UPl[...], V[t])

    loads[0].wait()
    store2(LI[...], LIh, LIl)
    loads[1].wait()
    V[0] = mm3_full(LIh[...], LIl[...], LS[0])
    ready(2, UP, UPh, UPl)
    W[0] = mm3_full(UPh[...], UPl[...], V[0])
    for h in range(2):
        UB[h, z] = pack(half(W[0], h))
    pl.semaphore_wait(barrier, 5)

    def tick(t, carry):
        steps = []

        def at(fn, *args):
            steps.append(functools.partial(fn, *args))

        def only(cond, fn, *args):
            def run():
                fn(*args)

            def go():
                pl.when(cond)(run)
            steps.append(go)

        one = t == 0
        for h in range(2):
            at(start, h)
            at(gather, h, 0)
            at(partial, h, t)
            for k in range(1, dm + 1):
                at(relay, h, k, 0)
                at(relay, h, k, 1)
                at(gather, h, k)
            at(give, h, t)
            at(solve, h, t)
            at(descend, h, t)
            for k in range(dm - 2, -2, -1):
                at(own, h, k)
            for k in range(dm - 2, -1, -1):
                at(hop, h, k, 0)
                at(hop, h, k, 1)
            if h == 0:
                at(leaf, 0, t, None)
                at(top, 0, t)
                only(t < ticks - 1, update, 0, t + 1)
            else:
                only(t > 0, leaf, 1, t - 1, False)
                only(t > 0, top, 1, t - 1)
                only(t > 0, update, 1, t)
        only(one, targets)
        for k in (0, 1, -1, 2, -2, 3, -3, 4):
            only(one, make_s, k)
        for w in range(nz):
            only(one, make_t, w)
        only(one, lambda: (loads[3].wait(), ready(4, PI, PIh, PIl)))
        only(one, lambda: (ready(5, IC, ICh, ICl), loads[6].wait()))
        only(one, lambda: store2(mmm(LIh[...], LIl[...], ICh[...], ICl[...]), Mh, Ml))
        only(one, lambda: store2(mmm(UPh[...], UPl[...], Mh[...], Ml[...]), M2h, M2l))
        only(one, static, 1)
        only(one, static, 2)
        only(one, lambda: ready(7, DN, DNh, DNl))
        for i in ORDER:
            steps[i]()
        return carry

    lax.fori_loop(0, ticks, tick, 0)
    leaf(1, ticks - 1, True)
    top(1, ticks - 1)
    for h in range(2):
        all_sends(dn_copy, h)
        mate_copy(PXS, PXR, px_sem, h).wait_send()
        mate_copy(SXS, SXR, sx_sem, h).wait_send()
        x_copy(h, ticks - 2).wait_send()
    for t in range(ticks):
        out_copy(PO, par_hbm, 1, t).wait()
        out_copy(LO, leaf_hbm, 0, t).wait()


def local(cfg, *args):
    n_panel, n_front, ticks = cfg
    li, pi, up, dn, ic, ls, ps, par, cnt, rows = args
    nz = n_front // 2
    dm = nz // 2
    N, C = ls.shape[3:]
    U = up.shape[2]
    Q = ic.shape[3]
    pr = U // 2
    v = pltpu.VMEM
    dma = pltpu.SemaphoreType.DMA
    scratch = [
        v((N, N), F32), v((N, N), F32), v((U, N), F32), v((N, U), F32), v((N, Q), F32),
        v((ticks, N, C), F32), v((ticks, N, C), F32),
        v((N, N), BF16), v((N, N), BF16), v((N, N), BF16), v((N, N), BF16),
        v((U, N), BF16), v((U, N), BF16), v((N, U), BF16), v((N, U), BF16),
        v((N, Q), BF16), v((N, Q), BF16), v((N, Q), BF16), v((N, Q), BF16), v((U, Q), BF16), v((U, Q), BF16),
        v((ticks, N, C), F32), v((ticks, U, C), F32),
        v((nz, N, U), BF16), v((nz, U, N), BF16), v((nz, U), jnp.int32),
        v((2, nz, pr, C), F32), v((2, 2, dm, pr, C), F32), v((2, 2, dm, pr, C), F32),
        v((2, N // 2, C), F32), v((2, N // 2, C), F32), v((2, N // 2, C), F32), v((2, N // 2, C), F32),
        v((2, Q // 2, C), F32), v((2, ticks - 1, Q // 2, C), F32),
        v((2, N, 2 * C), F32), v((2, 3, N, C), BF16), v((2, N, C), F32), v((2, pr, C), F32), v((2, U, C), F32),
        v((ticks, N, C), F32), v((ticks, N, C), F32),
        dma((8,)), dma((2, ticks)),
        dma((2, 2, dm, 2)), dma((2, 2, dm, 2)), dma((2, 2, dm, 2)), dma((2, 2, dm, 2)),
        dma((2, 2)), dma((2, 2)), dma((2,)), dma((2, ticks - 1)),
    ]
    hbm = pl.BlockSpec(memory_space=pl.ANY)
    smem = pl.BlockSpec(memory_space=pltpu.SMEM)
    return pl.pallas_call(
        functools.partial(kernel, cfg),
        out_shape=(jax.ShapeDtypeStruct(ls.shape, F32), jax.ShapeDtypeStruct(ps.shape, F32)),
        in_specs=[hbm] * 7 + [smem, smem, pl.BlockSpec(memory_space=pltpu.VMEM)],
        out_specs=(hbm, hbm),
        scratch_shapes=scratch,
        compiler_params=pltpu.CompilerParams(
            collective_id=0, has_side_effects=True, vmem_limit_bytes=62 * 1024 * 1024
        ),
        name="sweep",
    )(*args)


def solution(mesh):
    four = P("panel", "front", None, None)
    five = P("panel", "front", None, None, None)

    def step(*args):
        cfg = (mesh.shape["panel"], mesh.shape["front"], args[5].shape[2])
        return local(cfg, *args)

    return jax.shard_map(
        step,
        mesh=mesh,
        in_specs=(four,) * 5 + (five,) * 2 + (P("panel", None), P("panel", None), P("panel", None, None)),
        out_specs=(five, five),
        check_vma=False,
    )
```

```python
import functools

import jax
import jax.numpy as jnp
from jax import lax
from jax.experimental import pallas as pl
from jax.experimental.pallas import tpu as pltpu
from jax.sharding import PartitionSpec as P

F32 = jnp.float32
BF16 = jnp.bfloat16
MESH = pl.DeviceIdType.MESH
ORDER = (
    0, 62, 74, 85, 75, 63, 70, 59, 76, 69, 78, 72, 3, 1, 4, 79, 65, 6, 80, 7, 61, 68, 31, 71, 64, 67, 66, 60, 32, 5,
    9, 10, 8, 34, 84, 35, 11, 12, 13, 14, 37, 15, 73, 77, 38, 16, 40, 36, 41, 17, 39, 18, 43, 42, 44, 45, 22, 46, 23,
    19, 2, 47, 24, 25, 33, 48, 49, 20, 26, 50, 27, 83, 53, 54, 81, 21, 28, 55, 56, 82, 51, 57, 52, 58, 29, 30,
)


def dot(a, b):
    return jnp.dot(a, b, preferred_element_type=F32)


def split(x):
    hi = x.astype(BF16)
    return hi, (x - hi.astype(F32)).astype(BF16)


def kernel(
    cfg,
    li_hbm, pi_hbm, up_hbm, dn_hbm, ic_hbm, ls_hbm, ps_hbm, par_ref, cnt_ref, row_ref,
    leaf_hbm, par_hbm,
    LI, PI, UP, DN, IC, LS, PS,
    LIh, LIl, PIh, PIl, UPh, UPl, DNh, DNl, ICh, ICl, Mh, Ml, M2h, M2l,
    V, W, S, T, TG, UB, RB, SB, PXS, PXR, SXS, SXR, XS, XR, ACC, RG, PART, MINE, DOWN, LO, PO,
    ld_sem, st_sem, up_s, up_r, dn_s, dn_r, px_sem, sx_sem, x_s, x_r,
):
    n_panel, n_front, ticks = cfg
    nz = n_front // 2
    dm = nz // 2
    N, C = LS.shape[1:]
    U = UP.shape[0]
    Q = IC.shape[1]
    pr = U // 2
    nsub = 2
    cr = pr // 2
    sr = cr // nsub
    hc = C // 2
    panel = lax.axis_index("panel")
    front = lax.axis_index("front")
    z = front // 2
    core = lax.rem(front, 2)
    mate = front + 1 - 2 * core

    def zslot(d):
        return lax.rem(z + d + nz, nz)

    def zdev(d):
        return {"front": 2 * zslot(d) + core}

    ins = [(li_hbm.at[0, 0], LI), (ls_hbm.at[0, 0, 0], LS.at[0]), (up_hbm.at[0, 0], UP), (ps_hbm.at[0, 0], PS)]
    ins += [(pi_hbm.at[0, 0], PI), (ic_hbm.at[0, 0], IC), (ls_hbm.at[0, 0, 1:], LS.at[1:]), (dn_hbm.at[0, 0], DN)]
    loads = [pltpu.make_async_copy(src, dst, ld_sem.at[i]) for i, (src, dst) in enumerate(ins)]
    for c in loads:
        c.start()
    barrier = pltpu.get_barrier_semaphore()
    for who in (
        zdev(1), zdev(-1), {"front": mate},
        {"panel": lax.rem(panel + 1, n_panel)}, {"panel": lax.rem(panel + n_panel - 1, n_panel)},
    ):
        pl.semaphore_signal(barrier, inc=1, device_id=who, device_id_type=MESH)

    def low(shape):
        return lax.broadcasted_iota(jnp.int32, shape, 1) < hc

    def swap(x):
        return pltpu.roll(x, hc, 1)

    def half(x, h):
        return jnp.where(low(x.shape), x, swap(x)) if h == 0 else jnp.where(low(x.shape), swap(x), x)

    def pack(x):
        m = x.shape[0] // 2
        return jnp.where(low((m, C)), x[:m], x[m:])

    def unpack(p):
        m, s = low(p.shape), swap(p)
        return jnp.concatenate([jnp.where(m, p, s), jnp.where(m, s, p)], axis=0)

    def hilo(x):
        hi = x.astype(BF16).astype(F32)
        return jnp.where(low(x.shape), hi, x - hi)

    def fin(o):
        return o + swap(o)

    def mm3(ah, al, x):
        return fin(dot(ah, hilo(x).astype(BF16)) + dot(al, jnp.where(low(x.shape), x, 0.0).astype(BF16)))

    def mm3_full(ah, al, x):
        xh, xl = split(x)
        o = dot(ah, jnp.concatenate([xh, xl], axis=1))
        return o[:, :C] + o[:, C:] + dot(al, xh)

    def mmm(ah, al, bh, bl):
        return dot(ah, bh) + dot(ah, bl) + dot(al, bh)

    def store2(x, hi, lo):
        h, l = split(x)
        hi[...] = h
        lo[...] = l

    def in_half(d, c):
        return c == d

    def chunks(k, c):
        return [d for d in range(2) if k < dm - 1 or in_half(d, c)]

    def up_copy(h, d, k, c, q, back=0):
        sgn = 1 if d == 0 else -1
        ref = UB.at[h, zslot(-sgn * (k + back)), pl.ds(c * cr + q * sr, sr)]
        return pltpu.make_async_remote_copy(
            ref, ref, up_s.at[h, d, k, nsub * c + q], up_r.at[h, d, k, nsub * c + q], device_id=zdev(sgn), device_id_type=MESH
        )

    def dn_copy(h, d, k, c, q):
        at = pl.ds(c * cr + q * sr, sr)
        return pltpu.make_async_remote_copy(
            SB.at[h, d, k, at], RB.at[h, d, k, at], dn_s.at[h, d, k, nsub * c + q], dn_r.at[h, d, k, nsub * c + q],
            device_id=zdev(1 if d == 0 else -1), device_id_type=MESH,
        )

    def mate_copy(src, dst, sem, h):
        return pltpu.make_async_remote_copy(
            src.at[h], dst.at[h], sem.at[h, 0], sem.at[h, 1], device_id={"front": mate}, device_id_type=MESH
        )

    def x_copy(h, t):
        return pltpu.make_async_remote_copy(
            XS.at[h], XR.at[h, t], x_s.at[h], x_r.at[h, t],
            device_id={"panel": lax.rem(panel + 1, n_panel)}, device_id_type=MESH,
        )

    def all_sends(copy, h):
        for k in range(dm):
            for c in range(2):
                for d in chunks(k, c):
                    for q in range(nsub):
                        copy(h, d, k, c, q).wait_send()

    def out_copy(src, dst, i, t):
        return pltpu.make_async_copy(src.at[t], dst.at[0, 0, t], st_sem.at[i, t])

    def share(h, k):
        w = zslot(k)
        par = jnp.full((1, C), par_ref[0, 2 * w + core], jnp.int32)
        r = hilo(unpack(UB[h, w]))
        both = [jnp.where(par == who, r, 0.0).astype(BF16) for who in (front, mate)]
        return dot(S[w], jnp.concatenate(both, axis=1))

    def sel(h, k):
        w = zslot(k)
        par = par_ref[0, 2 * w + core]
        which = jnp.where(par == front, 0, jnp.where(par == mate, 1, 2))
        return pack(fin(dot(T[w], RG[h, which])))

    def start(h):
        for c in range(2):
            for d in range(2):
                for q in range(nsub):
                    up_copy(h, d, 0, c, q).start()

    def relay(h, k, c):
        for q in range(nsub):
            for d in chunks(k - 1, c):
                up_copy(h, d, k - 1, c, q, back=1).wait_recv()
                if k < dm and (k < dm - 1 or in_half(d, c)):
                    up_copy(h, d, k, c, q).start()

    def gather(h, k):
        if k == 0:
            ACC[h] = share(h, 0)
        elif k < dm:
            ACC[h] += share(h, -k) + share(h, k)
        else:
            ACC[h] += share(h, k)

    def arrived(h, t):
        return jnp.where(panel > 0, unpack(XR[h, t - 1]), 0.0)

    def partial(h, t):
        @pl.when(t == 0)
        def _():
            PART[h] = half(V[0], h)

        @pl.when(t > 0)
        def _():
            PART[h] = half(V[t], h) + mm3(Mh[...], Ml[...], arrived(h, t))

    def give(h, t):
        @pl.when(t > 0)
        def _():
            mate_copy(PXS, PXR, px_sem, h).wait_send()
        PXS[h] = pack(fin(ACC[h, :, C:]))
        mate_copy(PXS, PXR, px_sem, h).start()

    def solve(h, t):
        rhs = half(PS[t], h) - fin(ACC[h, :, :C])
        mate_copy(PXS, PXR, px_sem, h).wait_recv()
        solved = mm3(PIh[...], PIl[...], rhs - unpack(PXR[h]))

        @pl.when(t > 0)
        def _():
            mate_copy(SXS, SXR, sx_sem, h).wait_send()
        SXS[h] = pack(solved)
        mate_copy(SXS, SXR, sx_sem, h).start()
        RG[h, 0] = hilo(solved).astype(BF16)
        PO[t, :, h * hc : (h + 1) * hc] = solved[:, h * hc : (h + 1) * hc]
        if h == 1:
            out_copy(PO, par_hbm, 1, t).start()

    def descend(h, t):
        all_sends(up_copy, h)

        @pl.when(t > 0)
        def _():
            all_sends(dn_copy, h)
        mate_copy(SXS, SXR, sx_sem, h).wait_recv()
        RG[h, 1] = hilo(unpack(SXR[h])).astype(BF16)
        g = sel(h, dm)
        for d in range(2):
            at = pl.ds(d * cr, cr)
            SB[h, d, dm - 1, at] = g[d * cr : (d + 1) * cr]
            for q in range(nsub):
                dn_copy(h, d, dm - 1, d, q).start()

    def own(h, k):
        if k < 0:
            MINE[h] = sel(h, 0)
            return
        for d in range(2):
            SB[h, d, k] = sel(h, (k + 1) * (1 if d == 0 else -1))
        if k == dm - 2:
            for d in range(2):
                for q in range(nsub):
                    dn_copy(h, d, k, 1 - d, q).start()

    def hop(h, k, c):
        for q in range(nsub):
            at = pl.ds(c * cr + q * sr, sr)
            for d in chunks(k + 1, c):
                dn_copy(h, d, k + 1, c, q).wait_recv()
                SB[h, d, k, at] += RB[h, d, k + 1, at]
                dn_copy(h, d, k, c, q).start()

    def leaf(h, t, last):
        for c in range(2):
            for d in range(2):
                for q in range(nsub):
                    dn_copy(h, d, 0, c, q).wait_recv()
        down = unpack(MINE[h] + RB[h, 0, 0] + RB[h, 1, 0])
        DOWN[h] = down
        rest = PART[h, N - Q :] - mm3(DNh[N - Q :], DNl[N - Q :], down)

        def send():
            @pl.when(t > 0)
            def _():
                x_copy(h, t - 1).wait_send()
            XS[h] = pack(rest)
            x_copy(h, t).start()
        if last is None:
            pl.when(t < ticks - 1)(send)
        elif not last:
            send()
        LO[t, N - Q :, h * hc : (h + 1) * hc] = rest[:, h * hc : (h + 1) * hc]

    def top(h, t):
        rest = PART[h, : N - Q] - mm3(DNh[: N - Q], DNl[: N - Q], DOWN[h])
        LO[t, : N - Q, h * hc : (h + 1) * hc] = rest[:, h * hc : (h + 1) * hc]
        if h == 1:
            out_copy(LO, leaf_hbm, 0, t).start()

    def update(h, t):
        x_copy(h, t - 1).wait_recv()
        UB[h, z] = pack(half(W[t], h) + mm3(M2h[...], M2l[...], arrived(h, t)))

    def targets():
        k = lax.broadcasted_iota(jnp.int32, (1, U), 1)
        for w in range(nz):
            rows = row_ref[0, pl.ds(2 * w + core, 1), :]
            cnt = jnp.full((1, U), cnt_ref[0, 2 * w + core], jnp.int32)
            TG[pl.ds(w, 1), :] = jnp.where(k < cnt, rows, -1)
        RG[0, 2] = jnp.zeros((N, C), BF16)
        RG[1, 2] = jnp.zeros((N, C), BF16)

    def make_s(k):
        w = zslot(k)
        i = lax.broadcasted_iota(jnp.int32, (N, U), 0)
        S[w] = jnp.where(i == TG[pl.ds(w, 1), :], 1.0, 0.0).astype(BF16)

    def make_t(w):
        col = jnp.transpose(TG[...])[:, w : w + 1]
        i = lax.broadcasted_iota(jnp.int32, (U, N), 1)
        T[w] = jnp.where(i == col, 1.0, 0.0).astype(BF16)

    def ready(i, full, hi, lo):
        loads[i].wait()
        store2(full[...], hi, lo)

    def static(t):
        V[t] = mm3_full(LIh[...], LIl[...], LS[t])
        W[t] = mm3_full(UPh[...], UPl[...], V[t])

    loads[0].wait()
    store2(LI[...], LIh, LIl)
    loads[1].wait()
    V[0] = mm3_full(LIh[...], LIl[...], LS[0])
    ready(2, UP, UPh, UPl)
    W[0] = mm3_full(UPh[...], UPl[...], V[0])
    for h in range(2):
        UB[h, z] = pack(half(W[0], h))
    pl.semaphore_wait(barrier, 5)

    def tick(t, carry):
        steps = []

        def at(fn, *args):
            steps.append(functools.partial(fn, *args))

        def only(cond, fn, *args):
            def run():
                fn(*args)

            def go():
                pl.when(cond)(run)
            steps.append(go)

        one = t == 0
        for h in range(2):
            at(start, h)
            at(gather, h, 0)
            at(partial, h, t)
            for k in range(1, dm + 1):
                at(relay, h, k, 0)
                at(relay, h, k, 1)
                at(gather, h, k)
            at(give, h, t)
            at(solve, h, t)
            at(descend, h, t)
            for k in range(dm - 2, -2, -1):
                at(own, h, k)
            for k in range(dm - 2, -1, -1):
                at(hop, h, k, 0)
                at(hop, h, k, 1)
            if h == 0:
                at(leaf, 0, t, None)
                at(top, 0, t)
                only(t < ticks - 1, update, 0, t + 1)
            else:
                only(t > 0, leaf, 1, t - 1, False)
                only(t > 0, top, 1, t - 1)
                only(t > 0, update, 1, t)
        only(one, targets)
        for k in (0, 1, -1, 2, -2, 3, -3, 4):
            only(one, make_s, k)
        for w in range(nz):
            only(one, make_t, w)
        only(one, lambda: (loads[3].wait(), ready(4, PI, PIh, PIl)))
        only(one, lambda: (ready(5, IC, ICh, ICl), loads[6].wait()))
        only(one, lambda: store2(mmm(LIh[...], LIl[...], ICh[...], ICl[...]), Mh, Ml))
        only(one, lambda: store2(mmm(UPh[...], UPl[...], Mh[...], Ml[...]), M2h, M2l))
        only(one, static, 1)
        only(one, static, 2)
        only(one, lambda: ready(7, DN, DNh, DNl))
        for i in ORDER:
            steps[i]()
        return carry

    lax.fori_loop(0, ticks, tick, 0)
    leaf(1, ticks - 1, True)
    top(1, ticks - 1)
    for h in range(2):
        all_sends(dn_copy, h)
        mate_copy(PXS, PXR, px_sem, h).wait_send()
        mate_copy(SXS, SXR, sx_sem, h).wait_send()
        x_copy(h, ticks - 2).wait_send()
    for t in range(ticks):
        out_copy(PO, par_hbm, 1, t).wait()
        out_copy(LO, leaf_hbm, 0, t).wait()


def local(cfg, *args):
    n_panel, n_front, ticks = cfg
    li, pi, up, dn, ic, ls, ps, par, cnt, rows = args
    nz = n_front // 2
    dm = nz // 2
    N, C = ls.shape[3:]
    U = up.shape[2]
    Q = ic.shape[3]
    pr = U // 2
    v = pltpu.VMEM
    dma = pltpu.SemaphoreType.DMA
    scratch = [
        v((N, N), F32), v((N, N), F32), v((U, N), F32), v((N, U), F32), v((N, Q), F32),
        v((ticks, N, C), F32), v((ticks, N, C), F32),
        v((N, N), BF16), v((N, N), BF16), v((N, N), BF16), v((N, N), BF16),
        v((U, N), BF16), v((U, N), BF16), v((N, U), BF16), v((N, U), BF16),
        v((N, Q), BF16), v((N, Q), BF16), v((N, Q), BF16), v((N, Q), BF16), v((U, Q), BF16), v((U, Q), BF16),
        v((ticks, N, C), F32), v((ticks, U, C), F32),
        v((nz, N, U), BF16), v((nz, U, N), BF16), v((nz, U), jnp.int32),
        v((2, nz, pr, C), F32), v((2, 2, dm, pr, C), F32), v((2, 2, dm, pr, C), F32),
        v((2, N // 2, C), F32), v((2, N // 2, C), F32), v((2, N // 2, C), F32), v((2, N // 2, C), F32),
        v((2, Q // 2, C), F32), v((2, ticks - 1, Q // 2, C), F32),
        v((2, N, 2 * C), F32), v((2, 3, N, C), BF16), v((2, N, C), F32), v((2, pr, C), F32), v((2, U, C), F32),
        v((ticks, N, C), F32), v((ticks, N, C), F32),
        dma((8,)), dma((2, ticks)),
        dma((2, 2, dm, 4)), dma((2, 2, dm, 4)), dma((2, 2, dm, 4)), dma((2, 2, dm, 4)),
        dma((2, 2)), dma((2, 2)), dma((2,)), dma((2, ticks - 1)),
    ]
    hbm = pl.BlockSpec(memory_space=pl.ANY)
    smem = pl.BlockSpec(memory_space=pltpu.SMEM)
    return pl.pallas_call(
        functools.partial(kernel, cfg),
        out_shape=(jax.ShapeDtypeStruct(ls.shape, F32), jax.ShapeDtypeStruct(ps.shape, F32)),
        in_specs=[hbm] * 7 + [smem, smem, pl.BlockSpec(memory_space=pltpu.VMEM)],
        out_specs=(hbm, hbm),
        scratch_shapes=scratch,
        compiler_params=pltpu.CompilerParams(
            collective_id=0, has_side_effects=True, vmem_limit_bytes=62 * 1024 * 1024
        ),
        name="sweep",
    )(*args)


def solution(mesh):
    four = P("panel", "front", None, None)
    five = P("panel", "front", None, None, None)

    def step(*args):
        cfg = (mesh.shape["panel"], mesh.shape["front"], args[5].shape[2])
        return local(cfg, *args)

    return jax.shard_map(
        step,
        mesh=mesh,
        in_specs=(four,) * 5 + (five,) * 2 + (P("panel", None), P("panel", None), P("panel", None, None)),
        out_specs=(five, five),
        check_vma=False,
    )
```
